768 devices in a mesh: rep: 24 (over z, core), fsdp: 32 (over x, y).
Axes of the slice: x: 4, y: 8, z: 12, core: 2. Of those that a mesh axis runs over, the one named last changes fastest.
Arguments:
- grads: bfloat16 [24, 32, 768, 2048], P('rep', None, 'fsdp'), may hold values from -400 to 400
- momentum: float32 [32, 32, 24, 2048], P('fsdp', None, 'rep'), may hold values from -384 to 384
- owner: int32 [32], replicated, may hold values from 0 to 31, each once
Outputs:
- update: bfloat16 [32, 32, 24, 2048], P(None, 'fsdp', 'rep')
- momentum_out: float32 [32, 32, 24, 2048], P('fsdp', None, 'rep')
The draws below stay inside these ranges and needn't reach their ends.
Inputs may be any that keep to these rules, and one draw needn't show every extreme that they name: `owner`: every slot holds exactly one expert.
All inputs are finite; a program needn't handle non-finite values.
Results may differ from the reference program's by a relative error of at most 0.012.
Values may be sent and summed in bfloat16 or wider, within the bound.
No kernel may reach another device: no remote copies, remote signals or barrier semaphores. Data moves between devices by JAX's collectives and lax.ppermute only.
A program may use at most 32 MiB of HBM per device.

```python
import math
import jax
import jax.numpy as jnp
from jax import lax

D = 2048
FF = 768
ITERS = 2
EXPERTS = 32
REPLICAS = 24
BLOCKS = 32
SHARD_ROWS = 24


def draw_grads(key, part):
    key_noise, key_rows, key_cols = jax.random.split(jax.random.fold_in(key, 11), 3)
    row_scale = jnp.exp(jax.random.uniform(key_rows, (1, EXPERTS, FF, 1), jnp.float32, 0.0, math.log(10.0)))
    col_scale = jnp.exp(jax.random.uniform(key_cols, (1, EXPERTS, 1, D), jnp.float32, 0.0, math.log(10.0)))
    noise = jnp.clip(jax.random.normal(key_noise, (REPLICAS, EXPERTS, FF, D), jnp.float32), -4.0, 4.0)
    values = noise * row_scale * col_scale
    return jnp.clip(values, -400.0, 400.0).astype(jnp.bfloat16)


def block_levels(key, dims, shards, low, top_value):
    factor_of = 1.0
    for dim, parts in shards:
        draws = jax.random.uniform(jax.random.fold_in(jax.random.fold_in(key, 6), dim), (parts,), jnp.float32, low / len(shards), top_value / len(shards))
        factor_of = factor_of * jnp.repeat(jnp.exp(draws), dims[dim] // parts).reshape((-1,) + (1,) * (len(dims) - 1 - dim))
    return factor_of


def centred(key, dims, deviation, bound, cuts=(), kind=jnp.bfloat16):
    drawn = deviation * jax.random.normal(key, dims, jnp.float32)
    if cuts:
        drawn = drawn * block_levels(key, dims, cuts, -0.22, 0.18)
    return jnp.clip(drawn, -bound, bound).astype(kind)


def setup_inputs(seed: int = 0) -> dict:
    keys = jax.random.split(jax.random.key(seed), 4)
    return {
        "grads": draw_grads(jax.random.fold_in(keys[3], 71), 0),
        "momentum": centred(keys[1], (EXPERTS, BLOCKS, SHARD_ROWS, D), 60.0, 384.0, ((0, 32), (2, 24)), jnp.float32),
        "owner": jax.random.permutation(keys[2], EXPERTS).astype(jnp.int32),
    }


DECAY_RATE = 0.95
NEWTON_A = 3.4445
NEWTON_B = -4.775
NEWTON_C = 2.0315
EPSILON = 1e-07

def newton(nesterov):
    values = nesterov.astype(jnp.float32)
    frobenius = jnp.sqrt(jnp.sum(values * values))
    iterate = (values / (frobenius + EPSILON)).astype(jnp.bfloat16)
    result = values
    for iteration in range(ITERS):
        gram_matrix = jnp.dot(iterate, iterate.T, preferred_element_type=jnp.float32).astype(jnp.bfloat16)
        squared = jnp.dot(gram_matrix, gram_matrix, preferred_element_type=jnp.float32)
        polynomial = (NEWTON_B * gram_matrix.astype(jnp.float32) + NEWTON_C * squared).astype(jnp.bfloat16)
        result = NEWTON_A * iterate.astype(jnp.float32) + jnp.dot(polynomial, iterate, preferred_element_type=jnp.float32)
        iterate = result.astype(jnp.bfloat16)
    return result

def reference(grads, momentum, owner):
    full_moment = momentum.reshape(EXPERTS, FF, D)
    factor = math.sqrt(D)

    def one_expert(expert):
        replicas = lax.dynamic_index_in_dim(grads, expert, 1, keepdims=False)
        total = lax.optimization_barrier(jnp.sum(replicas.astype(jnp.float32), axis=0))
        slot = owner[expert]
        moment = lax.dynamic_index_in_dim(full_moment, slot, 0, keepdims=False)
        moment_new = DECAY_RATE * moment + total
        nesterov = (total + DECAY_RATE * moment_new).astype(jnp.bfloat16)
        update = (factor * newton(nesterov)).astype(jnp.bfloat16)
        return (update, moment_new)
    updates, moments = lax.map(one_expert, jnp.arange(EXPERTS, dtype=jnp.int32))
    moment_out = jnp.zeros((EXPERTS, FF, D), jnp.float32).at[owner].set(moments)
    return (updates.reshape(EXPERTS, BLOCKS, SHARD_ROWS, D), moment_out.reshape(EXPERTS, BLOCKS, SHARD_ROWS, D))
```

```python
import math

import jax
import jax.numpy as jnp
from jax import lax
from jax.sharding import PartitionSpec as P

DECAY_RATE = 0.95
NEWTON_A = 3.4445
NEWTON_B = -4.775
NEWTON_C = 2.0315
EPSILON = 1e-07

STRIDE = 3

F32 = jnp.float32
BF16 = jnp.bfloat16


def ring(replicas):
    other = [(r, r ^ 1) for r in range(replicas)]
    up = [(r, (r + 2) % replicas) for r in range(replicas)]
    down = [(r, (r - 2) % replicas) for r in range(replicas)]
    return other, up, down


def classes(replicas):
    chips = replicas // 2
    return [
        [2 * z + core for z in range(first, chips, STRIDE)]
        for first in range(STRIDE)
        for core in range(2)
    ]


def pick(array, index, axis):
    return lax.dynamic_index_in_dim(array, index, axis, keepdims=False)


def sum_rows(grads, replica, replicas):
    experts, _, width = grads.shape
    other, up, down = ring(replicas)
    core = replica % 2
    kind = (replica // 2) % STRIDE
    rows = grads.transpose(1, 0, 2).reshape(replicas // (2 * STRIDE), STRIDE, 2, experts, width)
    mine = pick(rows, core, 2)
    theirs = lax.ppermute(pick(rows, 1 - core, 2), "rep", other)

    def chip_sum(which):
        return pick(mine, which, 1).astype(F32) + pick(theirs, which, 1).astype(F32)

    from_below = lax.ppermute(chip_sum((kind + 1) % STRIDE).astype(BF16), "rep", up)
    from_above = lax.ppermute(chip_sum((kind + 2) % STRIDE).astype(BF16), "rep", down)
    cluster = (chip_sum(kind) + from_below.astype(F32) + from_above.astype(F32)).astype(BF16)
    return lax.all_to_all(cluster, "rep", 0, 0, tiled=True, axis_index_groups=classes(replicas))


def gather_rows(rows, replicas):
    other, up, down = ring(replicas)
    own = lax.all_gather(rows, "rep", axis=0, tiled=True, axis_index_groups=classes(replicas))
    below = lax.ppermute(own, "rep", up)
    above = lax.ppermute(own, "rep", down)
    pieces = [own, below, above]
    return jnp.concatenate(pieces + [lax.ppermute(piece, "rep", other) for piece in pieces], axis=0)


def newton_rows(whole, rows, first_row):
    count = rows.shape[0]
    raw = lax.dot_general(whole, whole, (((1,), (1,)), ((), ())), preferred_element_type=F32)
    size = raw.shape[0]
    diagonal = lax.broadcasted_iota(jnp.int32, (size, size), 0) == lax.broadcasted_iota(jnp.int32, (size, size), 1)
    scale = 1.0 / (jnp.sqrt(jnp.sum(jnp.where(diagonal, raw, 0.0))) + EPSILON)
    gram = (raw * scale * scale).astype(BF16)

    def dot(a, b):
        return jnp.dot(a, b, preferred_element_type=F32)

    def own(matrix):
        return lax.dynamic_slice_in_dim(matrix, first_row, count, 0)

    poly = (NEWTON_B * gram.astype(F32) + NEWTON_C * dot(gram, gram)).astype(BF16)
    mixed = dot(gram, poly).astype(BF16)
    gram_next = (
        NEWTON_A * NEWTON_A * gram.astype(F32) + 2.0 * NEWTON_A * mixed.astype(F32) + dot(mixed, poly)
    ).astype(BF16)
    own_gram = own(gram_next)
    own_poly = (NEWTON_B * own_gram.astype(F32) + NEWTON_C * dot(own_gram, gram_next)).astype(BF16)
    weights = NEWTON_A * (own(poly).astype(F32) + own_poly.astype(F32)) + dot(own_poly, poly)
    return scale * (NEWTON_A * NEWTON_A * rows.astype(F32) + dot(weights.astype(BF16), whole))


def on_device(grads, momentum, owner):
    slots = lax.axis_size("fsdp")
    replicas = lax.axis_size("rep")
    replica = lax.axis_index("rep")
    width = grads.shape[-1]
    lanes = math.gcd(width, 128)
    tiled = (slots, width // lanes, lanes)

    terms = sum_rows(grads[0], replica, replicas)
    onehot = (owner[None, :] == jnp.arange(slots, dtype=jnp.int32)[:, None]).astype(BF16)
    every = jnp.concatenate([onehot] * terms.shape[0], axis=1)
    outgoing = jnp.dot(every, terms.reshape(-1, width), preferred_element_type=F32)
    grad_rows = lax.all_to_all(outgoing.reshape(tiled), "fsdp", split_axis=0, concat_axis=0, tiled=True)
    moment_new = DECAY_RATE * momentum.reshape(tiled) + grad_rows
    nesterov = (grad_rows + DECAY_RATE * moment_new).astype(BF16).reshape(slots, width)

    whole = gather_rows(nesterov, replicas)
    result = newton_rows(whole, nesterov, (replica // (2 * STRIDE)) * slots)
    update_rows = (math.sqrt(width) * result).astype(BF16)

    returning = lax.all_to_all(update_rows.reshape(tiled), "fsdp", split_axis=0, concat_axis=0, tiled=True)
    updates = jnp.einsum(
        "se,sd->ed", onehot, returning.reshape(slots, width), preferred_element_type=F32
    ).astype(BF16)
    return (updates[:, None, None], moment_new.reshape(momentum.shape))


def solution(mesh):
    placed = (P("rep", None, "fsdp", None), P("fsdp", None, "rep", None), P())
    return jax.shard_map(
        on_device,
        mesh=mesh,
        in_specs=placed,
        out_specs=(P(None, "fsdp", "rep", None), P("fsdp", None, "rep", None)),
        check_vma=False,
    )
```

```python
import math

import jax
import jax.numpy as jnp
from jax import lax
from jax.experimental import pallas as pl
from jax.experimental.pallas import tpu as pltpu
from jax.sharding import PartitionSpec as P

DECAY_RATE = 0.95
NEWTON_A = 3.4445
NEWTON_B = -4.775
NEWTON_C = 2.0315
EPSILON = 1e-07

STRIDE = 3

F32 = jnp.float32
BF16 = jnp.bfloat16

SCALARS = pl.BlockSpec(memory_space=pltpu.SMEM)
VECTORS = pl.BlockSpec(memory_space=pltpu.VMEM)


def grant(mebibytes):
    return pltpu.CompilerParams(vmem_limit_bytes=mebibytes * 2**20)


def shift(chips, replicas):
    return [(r, (r + 2 * chips) % replicas) for r in range(replicas)]


def other_core(replicas):
    return [(r, r ^ 1) for r in range(replicas)]


def classes(replicas):
    chips = replicas // 2
    return [
        [2 * z + core for z in range(first, chips, STRIDE)]
        for first in range(STRIDE)
        for core in range(2)
    ]


def pick(array, index, axis):
    return lax.dynamic_index_in_dim(array, index, axis, keepdims=False)


def chip_sums_kernel(replica_ref, mine_ref, theirs_ref, up_ref, down_ref):
    core = lax.rem(replica_ref[0], 2)
    kind = lax.rem(lax.div(replica_ref[0], 2), STRIDE)
    for step, out_ref in ((1, up_ref), (2, down_ref)):
        there = lax.rem(kind + step, STRIDE)
        for n in range(out_ref.shape[0]):
            out_ref[n] = (mine_ref[n, there, core].astype(F32) + theirs_ref[n, there].astype(F32)).astype(BF16)


def cluster_sums_kernel(replica_ref, mine_ref, theirs_ref, below_ref, above_ref, *out_refs):
    core = lax.rem(replica_ref[0], 2)
    chip = lax.div(replica_ref[0], 2)
    kind, place = lax.rem(chip, STRIDE), lax.div(chip, STRIDE)
    for step, out_ref in enumerate(out_refs):
        n = lax.rem(place + step, len(out_refs))
        total = mine_ref[n, kind, core].astype(F32) + theirs_ref[n, kind].astype(F32)
        out_ref[...] = (total + below_ref[n].astype(F32) + above_ref[n].astype(F32)).astype(BF16)


def place_kernel(owner_ref, *refs):
    parts, out_ref = refs[:-1], refs[-1]
    slots, tiles, lanes = out_ref.shape
    slot = lax.broadcasted_iota(jnp.int32, (slots, slots), 0)
    onehot = jnp.where(slot == owner_ref[...], 1.0, 0.0).astype(BF16)
    total = product(onehot, parts[0][...])
    for part in parts[1:]:
        total += product(onehot, part[...])
    for tile in range(tiles):
        out_ref[:, tile, :] = total[:, tile * lanes : (tile + 1) * lanes]


def sum_rows(grads, owner, replica, replicas, lanes):
    experts, _, width = grads.shape
    members = replicas // (2 * STRIDE)
    here = replica.reshape(1)
    mine = grads.transpose(1, 0, 2).reshape(members, STRIDE, 2, experts, width)
    theirs = lax.ppermute(pick(mine, 1 - replica % 2, 2), "rep", other_core(replicas))
    some = jax.ShapeDtypeStruct((members, experts, width), BF16)
    up, down = pl.pallas_call(
        chip_sums_kernel,
        out_shape=(some, some),
        in_specs=[SCALARS, VECTORS, VECTORS],
        out_specs=(VECTORS, VECTORS),
        compiler_params=grant(12),
        name="chip_sums",
    )(here, mine, theirs)
    below = lax.ppermute(up, "rep", shift(1, replicas))
    above = lax.ppermute(down, "rep", shift(-1, replicas))
    sums = pl.pallas_call(
        cluster_sums_kernel,
        out_shape=(jax.ShapeDtypeStruct((experts, width), BF16),) * members,
        in_specs=[SCALARS] + [VECTORS] * 4,
        out_specs=(VECTORS,) * members,
        compiler_params=grant(12),
        name="cluster_sums",
    )(here, mine, theirs, below, above)
    parts = [sums[0]]
    for step in sorted(range(1, members), key=lambda n: abs(2 * n - members), reverse=True):
        parts.append(lax.ppermute(sums[step], "rep", shift(STRIDE * step, replicas)))
    return pl.pallas_call(
        place_kernel,
        out_shape=jax.ShapeDtypeStruct((experts, width // lanes, lanes), F32),
        in_specs=[VECTORS] * (1 + members),
        out_specs=VECTORS,
        compiler_params=grant(4),
        name="place",
    )(owner.reshape(1, -1), *parts)


def gather_rows(rows, replicas):
    own = lax.all_gather(rows, "rep", axis=0, tiled=True, axis_index_groups=classes(replicas))
    below = lax.ppermute(own, "rep", shift(1, replicas))
    above = lax.ppermute(own, "rep", shift(-1, replicas))
    pieces = [own, below, above]
    return pieces + [lax.ppermute(piece, "rep", other_core(replicas)) for piece in pieces]


def product(a, b):
    return lax.dot_general(a, b, (((1,), (0,)), ((), ())), preferred_element_type=F32)


def newton_kernel(count, factor, first_ref, *refs):
    pieces, (out_ref, x_ref, raw_ref, gram_ref, poly_ref, mixed_ref, next_ref) = refs[:-7], refs[-7:]
    height = pieces[0].shape[0]
    for n, piece in enumerate(pieces):
        x_ref[pl.ds(n * height, height), :] = piece[...]
    size = x_ref.shape[0]
    step = 2 * height
    blocks = [pl.ds(n * step, step) for n in range(size // step)]
    diagonal = lax.broadcasted_iota(jnp.int32, (step, step), 0) == lax.broadcasted_iota(jnp.int32, (step, step), 1)
    trace = jnp.float32(0.0)
    for n, block in enumerate(blocks):
        raw = lax.dot_general(x_ref[block, :], x_ref[...], (((1,), (1,)), ((), ())), preferred_element_type=F32)
        raw_ref[block, :] = raw
        trace += jnp.sum(jnp.where(diagonal, raw[:, n * step : (n + 1) * step], 0.0))
    scale = 1.0 / (jnp.sqrt(trace) + EPSILON)
    for block in blocks:
        gram_ref[block, :] = (raw_ref[block, :] * scale * scale).astype(BF16)
    for block in blocks:
        squared = product(gram_ref[block, :], gram_ref[...])
        poly_ref[block, :] = (NEWTON_B * gram_ref[block, :].astype(F32) + NEWTON_C * squared).astype(BF16)
    for block in blocks:
        mixed_ref[block, :] = product(gram_ref[block, :], poly_ref[...]).astype(BF16)
    for block in blocks:
        own = NEWTON_A * NEWTON_A * gram_ref[block, :].astype(F32) + 2.0 * NEWTON_A * mixed_ref[block, :].astype(F32)
        next_ref[block, :] = (own + product(mixed_ref[block, :], poly_ref[...])).astype(BF16)
    rows = pl.ds(pl.multiple_of(first_ref[0], count), count)
    own_gram = next_ref[rows, :]
    own_poly = NEWTON_B * own_gram.astype(F32) + NEWTON_C * product(own_gram, next_ref[...])
    own_poly = own_poly.astype(BF16)
    weights = NEWTON_A * (poly_ref[rows, :].astype(F32) + own_poly.astype(F32)) + product(own_poly, poly_ref[...])
    result = NEWTON_A * NEWTON_A * x_ref[rows, :].astype(F32) + product(weights.astype(BF16), x_ref[...])
    out_ref[...] = (factor * scale * result).astype(BF16)


def newton_rows(pieces, count, first_row, factor):
    height, width = pieces[0].shape
    size = height * len(pieces)
    square = pltpu.VMEM((size, size), BF16)
    return pl.pallas_call(
        lambda *refs: newton_kernel(count, factor, *refs),
        out_shape=jax.ShapeDtypeStruct((count, width), BF16),
        in_specs=[SCALARS] + [VECTORS] * len(pieces),
        out_specs=VECTORS,
        scratch_shapes=[pltpu.VMEM((size, width), BF16), pltpu.VMEM((size, size), F32), square, square, square, square],
        compiler_params=grant(20),
        name="newton",
    )(first_row.reshape(1), *pieces)


def on_device(grads, momentum, owner):
    slots = lax.axis_size("fsdp")
    replicas = lax.axis_size("rep")
    replica = lax.axis_index("rep")
    width = grads.shape[-1]
    lanes = math.gcd(width, 128)
    tiled = (slots, width // lanes, lanes)

    outgoing = sum_rows(grads[0], owner, replica, replicas, lanes)
    grad_rows = lax.all_to_all(outgoing, "fsdp", split_axis=0, concat_axis=0, tiled=True)
    moment_new = DECAY_RATE * momentum.reshape(tiled) + grad_rows
    nesterov = (grad_rows + DECAY_RATE * moment_new).astype(BF16).reshape(slots, width)

    pieces = gather_rows(nesterov, replicas)
    update_rows = newton_rows(pieces, slots, (replica // (2 * STRIDE)) * slots, math.sqrt(width))

    returning = lax.all_to_all(update_rows.reshape(tiled), "fsdp", split_axis=0, concat_axis=0, tiled=True)
    onehot = (owner[None, :] == jnp.arange(slots, dtype=jnp.int32)[:, None]).astype(BF16)
    updates = jnp.einsum(
        "se,sd->ed", onehot, returning.reshape(slots, width), preferred_element_type=F32
    ).astype(BF16)
    return (updates[:, None, None], moment_new.reshape(momentum.shape))


def solution(mesh):
    placed = (P("rep", None, "fsdp", None), P("fsdp", None, "rep", None), P())
    return jax.shard_map(
        on_device,
        mesh=mesh,
        in_specs=placed,
        out_specs=(P(None, "fsdp", "rep", None), P("fsdp", None, "rep", None)),
        check_vma=False,
    )
```

```python
import math

import jax
import jax.numpy as jnp
from jax import lax
from jax.experimental import pallas as pl
from jax.experimental.pallas import tpu as pltpu
from jax.sharding import PartitionSpec as P

DECAY_RATE = 0.95
NEWTON_A = 3.4445
NEWTON_B = -4.775
NEWTON_C = 2.0315
EPSILON = 1e-07

STRIDE = 3

F32 = jnp.float32
BF16 = jnp.bfloat16

SCALARS = pl.BlockSpec(memory_space=pltpu.SMEM)
VECTORS = pl.BlockSpec(memory_space=pltpu.VMEM)


def grant(mebibytes):
    return pltpu.CompilerParams(vmem_limit_bytes=mebibytes * 2**20)


def shift(chips, replicas):
    return [(r, (r + 2 * chips) % replicas) for r in range(replicas)]


def other_core(replicas):
    return [(r, r ^ 1) for r in range(replicas)]


def classes(replicas):
    chips = replicas // 2
    return [
        [2 * z + core for z in range(first, chips, STRIDE)]
        for first in range(STRIDE)
        for core in range(2)
    ]


def pick(array, index, axis):
    return lax.dynamic_index_in_dim(array, index, axis, keepdims=False)


def chip_sums_kernel(replica_ref, mine_ref, theirs_ref, up_ref, down_ref):
    core = lax.rem(replica_ref[0], 2)
    kind = lax.rem(lax.div(replica_ref[0], 2), STRIDE)
    for step, out_ref in ((1, up_ref), (2, down_ref)):
        there = lax.rem(kind + step, STRIDE)
        for n in range(out_ref.shape[0]):
            out_ref[n] = (mine_ref[n, there, core].astype(F32) + theirs_ref[n, there].astype(F32)).astype(BF16)


def cluster_sums_kernel(replica_ref, owner_ref, mine_ref, theirs_ref, below_ref, above_ref, out_ref, row_ref):
    core = lax.rem(replica_ref[0], 2)
    kind = lax.rem(lax.div(replica_ref[0], 2), STRIDE)
    experts, tiles, lanes = row_ref.shape
    for n in range(out_ref.shape[0]):
        total = mine_ref[n, kind, core].astype(F32) + theirs_ref[n, kind].astype(F32)
        total += below_ref[n].astype(F32) + above_ref[n].astype(F32)
        for tile in range(tiles):
            row_ref[:, tile, :] = total[:, tile * lanes : (tile + 1) * lanes]
        for expert in range(experts):
            out_ref[n, owner_ref[expert]] = row_ref[expert].astype(BF16)


def momentum_kernel(terms_ref, moment_ref, moment_out_ref, rows_ref, row_ref):
    total = terms_ref[0].astype(F32)
    for n in range(1, terms_ref.shape[0]):
        total += terms_ref[n].astype(F32)
    moment = DECAY_RATE * moment_ref[...] + total
    moment_out_ref[...] = moment
    row_ref[...] = total + DECAY_RATE * moment
    _, tiles, lanes = row_ref.shape
    for tile in range(tiles):
        rows_ref[:, tile * lanes : (tile + 1) * lanes] = row_ref[:, tile, :].astype(BF16)


def cluster_sums(grads, owner, replica, replicas, lanes):
    experts, _, width = grads.shape
    members = replicas // (2 * STRIDE)
    here = replica.reshape(1)
    mine = grads.transpose(1, 0, 2).reshape(members, STRIDE, 2, experts, width)
    theirs = lax.ppermute(pick(mine, 1 - replica % 2, 2), "rep", other_core(replicas))
    some = jax.ShapeDtypeStruct((members, experts, width), BF16)
    up, down = pl.pallas_call(
        chip_sums_kernel,
        out_shape=(some, some),
        in_specs=[SCALARS, VECTORS, VECTORS],
        out_specs=(VECTORS, VECTORS),
        compiler_params=grant(12),
        name="chip_sums",
    )(here, mine, theirs)
    below = lax.ppermute(up, "rep", shift(1, replicas))
    above = lax.ppermute(down, "rep", shift(-1, replicas))
    tiles = (experts, width // lanes, lanes)
    return pl.pallas_call(
        cluster_sums_kernel,
        out_shape=jax.ShapeDtypeStruct((members, *tiles), BF16),
        in_specs=[SCALARS] * 2 + [VECTORS] * 4,
        out_specs=VECTORS,
        scratch_shapes=[pltpu.VMEM(tiles, F32)],
        compiler_params=grant(12),
        name="cluster_sums",
    )(here, owner, mine, theirs, below, above)


def momentum_rows(terms, moment):
    slots, tiles, lanes = moment.shape
    return pl.pallas_call(
        momentum_kernel,
        out_shape=(jax.ShapeDtypeStruct(moment.shape, F32), jax.ShapeDtypeStruct((slots, tiles * lanes), BF16)),
        in_specs=[VECTORS, VECTORS],
        out_specs=(VECTORS, VECTORS),
        scratch_shapes=[pltpu.VMEM(moment.shape, F32)],
        compiler_params=grant(4),
        name="momentum",
    )(terms, moment)


def gather_rows(rows, replicas):
    own = lax.all_gather(rows, "rep", axis=0, tiled=True, axis_index_groups=classes(replicas))
    below = lax.ppermute(own, "rep", shift(1, replicas))
    above = lax.ppermute(own, "rep", shift(-1, replicas))
    pieces = [own, below, above]
    return pieces + [lax.ppermute(piece, "rep", other_core(replicas)) for piece in pieces]


def product(a, b):
    return lax.dot_general(a, b, (((1,), (0,)), ((), ())), preferred_element_type=F32)


def newton_kernel(count, factor, first_ref, *refs):
    pieces, (out_ref, x_ref, raw_ref, gram_ref, poly_ref, mixed_ref, next_ref) = refs[:-7], refs[-7:]
    height = pieces[0].shape[0]
    for n, piece in enumerate(pieces):
        x_ref[pl.ds(n * height, height), :] = piece[...]
    size = x_ref.shape[0]
    step = 2 * height
    blocks = [pl.ds(n * step, step) for n in range(size // step)]
    diagonal = lax.broadcasted_iota(jnp.int32, (step, step), 0) == lax.broadcasted_iota(jnp.int32, (step, step), 1)
    trace = jnp.float32(0.0)
    for n, block in enumerate(blocks):
        raw = lax.dot_general(x_ref[block, :], x_ref[...], (((1,), (1,)), ((), ())), preferred_element_type=F32)
        raw_ref[block, :] = raw
        trace += jnp.sum(jnp.where(diagonal, raw[:, n * step : (n + 1) * step], 0.0))
    scale = 1.0 / (jnp.sqrt(trace) + EPSILON)
    for block in blocks:
        gram_ref[block, :] = (raw_ref[block, :] * scale * scale).astype(BF16)
    for block in blocks:
        squared = product(gram_ref[block, :], gram_ref[...])
        poly_ref[block, :] = (NEWTON_B * gram_ref[block, :].astype(F32) + NEWTON_C * squared).astype(BF16)
    for block in blocks:
        mixed_ref[block, :] = product(gram_ref[block, :], poly_ref[...]).astype(BF16)
    for block in blocks:
        own = NEWTON_A * NEWTON_A * gram_ref[block, :].astype(F32) + 2.0 * NEWTON_A * mixed_ref[block, :].astype(F32)
        next_ref[block, :] = (own + product(mixed_ref[block, :], poly_ref[...])).astype(BF16)
    rows = pl.ds(pl.multiple_of(first_ref[0], count), count)
    own_gram = next_ref[rows, :]
    own_poly = NEWTON_B * own_gram.astype(F32) + NEWTON_C * product(own_gram, next_ref[...])
    own_poly = own_poly.astype(BF16)
    weights = NEWTON_A * (poly_ref[rows, :].astype(F32) + own_poly.astype(F32)) + product(own_poly, poly_ref[...])
    result = NEWTON_A * NEWTON_A * x_ref[rows, :].astype(F32) + product(weights.astype(BF16), x_ref[...])
    out_ref[...] = (factor * scale * result).astype(BF16)


def newton_rows(pieces, count, first_row, factor):
    height, width = pieces[0].shape
    size = height * len(pieces)
    square = pltpu.VMEM((size, size), BF16)
    return pl.pallas_call(
        lambda *refs: newton_kernel(count, factor, *refs),
        out_shape=jax.ShapeDtypeStruct((count, width), BF16),
        in_specs=[SCALARS] + [VECTORS] * len(pieces),
        out_specs=VECTORS,
        scratch_shapes=[pltpu.VMEM((size, width), BF16), pltpu.VMEM((size, size), F32), square, square, square, square],
        compiler_params=grant(20),
        name="newton",
    )(first_row.reshape(1), *pieces)


def on_device(grads, momentum, owner):
    slots = lax.axis_size("fsdp")
    replicas = lax.axis_size("rep")
    replica = lax.axis_index("rep")
    width = grads.shape[-1]
    lanes = math.gcd(width, 128)
    tiled = (slots, width // lanes, lanes)

    sums = cluster_sums(grads[0], owner, replica, replicas, lanes)
    members = sums.shape[0]
    groups = [[r * slots + s for r in group for s in range(slots)] for group in classes(replicas)]
    terms = lax.all_to_all(
        sums.reshape(members * slots, *tiled[1:]), ("rep", "fsdp"), 0, 0, axis_index_groups=groups, tiled=True
    )
    moment_new, nesterov = momentum_rows(terms.reshape(members, *tiled), momentum.reshape(tiled))

    pieces = gather_rows(nesterov, replicas)
    update_rows = newton_rows(pieces, slots, (replica // (2 * STRIDE)) * slots, math.sqrt(width))

    returning = lax.all_to_all(update_rows.reshape(tiled), "fsdp", split_axis=0, concat_axis=0, tiled=True)
    onehot = (owner[None, :] == jnp.arange(slots, dtype=jnp.int32)[:, None]).astype(BF16)
    updates = jnp.einsum(
        "se,sd->ed", onehot, returning.reshape(slots, width), preferred_element_type=F32
    ).astype(BF16)
    return (updates[:, None, None], moment_new.reshape(momentum.shape))


def solution(mesh):
    placed = (P("rep", None, "fsdp", None), P("fsdp", None, "rep", None), P())
    return jax.shard_map(
        on_device,
        mesh=mesh,
        in_specs=placed,
        out_specs=(P(None, "fsdp", "rep", None), P("fsdp", None, "rep", None)),
        check_vma=False,
    )
```

```python
import math

import jax
import jax.numpy as jnp
from jax import lax
from jax.experimental import pallas as pl
from jax.experimental.pallas import tpu as pltpu
from jax.sharding import PartitionSpec as P

DECAY_RATE = 0.95
NEWTON_A = 3.4445
NEWTON_B = -4.775
NEWTON_C = 2.0315
EPSILON = 1e-07

STRIDE = 3

F32 = jnp.float32
BF16 = jnp.bfloat16

SCALARS = pl.BlockSpec(memory_space=pltpu.SMEM)
VECTORS = pl.BlockSpec(memory_space=pltpu.VMEM)


def grant(mebibytes):
    return pltpu.CompilerParams(vmem_limit_bytes=mebibytes * 2**20)


def neighbours(turn, replicas):
    return [(r, (r + 2 - 4 * ((r + turn) % 2)) % replicas) for r in range(replicas)]


def other_core(replicas):
    return [(r, r ^ 1) for r in range(replicas)]


def classes(replicas):
    chips = replicas // 2
    return [
        [2 * z + core for z in range(first, chips, STRIDE)]
        for first in range(STRIDE)
        for core in range(2)
    ]


def pick(array, index, axis):
    return lax.dynamic_index_in_dim(array, index, axis, keepdims=False)


def chip_sums_kernel(replica_ref, mine_ref, theirs_ref, *out_refs):
    core = lax.rem(replica_ref[0], 2)
    kind = lax.rem(lax.div(replica_ref[0], 2), STRIDE)
    for step, out_ref in zip((1 + core, 2 - core), out_refs, strict=True):
        there = lax.rem(kind + step, STRIDE)
        for n in range(out_ref.shape[0]):
            out_ref[n] = (mine_ref[n, there, core].astype(F32) + theirs_ref[n, there].astype(F32)).astype(BF16)


def cluster_sums_kernel(replica_ref, owner_ref, mine_ref, theirs_ref, first_ref, second_ref, out_ref, row_ref):
    core = lax.rem(replica_ref[0], 2)
    kind = lax.rem(lax.div(replica_ref[0], 2), STRIDE)
    experts, tiles, lanes = row_ref.shape
    for n in range(out_ref.shape[0]):
        total = mine_ref[n, kind, core].astype(F32) + theirs_ref[n, kind].astype(F32)
        total += first_ref[n].astype(F32) + second_ref[n].astype(F32)
        for tile in range(tiles):
            row_ref[:, tile, :] = total[:, tile * lanes : (tile + 1) * lanes]
        for expert in range(experts):
            out_ref[n, owner_ref[expert]] = row_ref[expert].astype(BF16)


def momentum_kernel(terms_ref, moment_ref, moment_out_ref, rows_ref, row_ref):
    total = terms_ref[0].astype(F32)
    for n in range(1, terms_ref.shape[0]):
        total += terms_ref[n].astype(F32)
    moment = DECAY_RATE * moment_ref[...] + total
    moment_out_ref[...] = moment
    row_ref[...] = total + DECAY_RATE * moment
    _, tiles, lanes = row_ref.shape
    for tile in range(tiles):
        rows_ref[:, tile * lanes : (tile + 1) * lanes] = row_ref[:, tile, :].astype(BF16)


def cluster_sums(grads, owner, replica, replicas, lanes):
    experts, _, width = grads.shape
    members = replicas // (2 * STRIDE)
    here = replica.reshape(1)
    mine = grads.transpose(1, 0, 2).reshape(members, STRIDE, 2, experts, width)
    theirs = lax.ppermute(pick(mine, 1 - replica % 2, 2), "rep", other_core(replicas))
    some = jax.ShapeDtypeStruct((members, experts, width), BF16)
    outward = pl.pallas_call(
        chip_sums_kernel,
        out_shape=(some, some),
        in_specs=[SCALARS, VECTORS, VECTORS],
        out_specs=(VECTORS, VECTORS),
        compiler_params=grant(12),
        name="chip_sums",
    )(here, mine, theirs)
    inward = [lax.ppermute(sums, "rep", neighbours(turn, replicas)) for turn, sums in enumerate(outward)]
    tiles = (experts, width // lanes, lanes)
    return pl.pallas_call(
        cluster_sums_kernel,
        out_shape=jax.ShapeDtypeStruct((members, *tiles), BF16),
        in_specs=[SCALARS] * 2 + [VECTORS] * 4,
        out_specs=VECTORS,
        scratch_shapes=[pltpu.VMEM(tiles, F32)],
        compiler_params=grant(12),
        name="cluster_sums",
    )(here, owner, mine, theirs, *inward)


def momentum_rows(terms, moment):
    slots, tiles, lanes = moment.shape
    return pl.pallas_call(
        momentum_kernel,
        out_shape=(jax.ShapeDtypeStruct(moment.shape, F32), jax.ShapeDtypeStruct((slots, tiles * lanes), BF16)),
        in_specs=[VECTORS, VECTORS],
        out_specs=(VECTORS, VECTORS),
        scratch_shapes=[pltpu.VMEM(moment.shape, F32)],
        compiler_params=grant(4),
        name="momentum",
    )(terms, moment)


def gather_rows(rows, replicas):
    own = lax.all_gather(rows, "rep", axis=0, tiled=True, axis_index_groups=classes(replicas))
    pieces = [own] + [lax.ppermute(own, "rep", neighbours(turn, replicas)) for turn in range(2)]
    return pieces + [lax.ppermute(piece, "rep", other_core(replicas)) for piece in pieces]


def product(a, b):
    return lax.dot_general(a, b, (((1,), (0,)), ((), ())), preferred_element_type=F32)


def newton_kernel(count, factor, first_ref, *refs):
    pieces, (out_ref, x_ref, raw_ref, gram_ref, poly_ref) = refs[:-5], refs[-5:]
    height = pieces[0].shape[0]
    for n, piece in enumerate(pieces):
        x_ref[pl.ds(n * height, height), :] = piece[...]
    size = x_ref.shape[0]
    step = 2 * height
    blocks = [pl.ds(n * step, step) for n in range(size // step)]
    diagonal = lax.broadcasted_iota(jnp.int32, (step, step), 0) == lax.broadcasted_iota(jnp.int32, (step, step), 1)
    trace = jnp.float32(0.0)
    for n, block in enumerate(blocks):
        raw = lax.dot_general(x_ref[block, :], x_ref[...], (((1,), (1,)), ((), ())), preferred_element_type=F32)
        raw_ref[block, :] = raw
        trace += jnp.sum(jnp.where(diagonal, raw[:, n * step : (n + 1) * step], 0.0))
    scale = 1.0 / (jnp.sqrt(trace) + EPSILON)
    for block in blocks:
        gram_ref[block, :] = (raw_ref[block, :] * scale * scale).astype(BF16)
    for block in blocks:
        squared = product(gram_ref[block, :], gram_ref[...])
        poly_ref[block, :] = (NEWTON_B * gram_ref[block, :].astype(F32) + NEWTON_C * squared).astype(BF16)
    rows = pl.ds(pl.multiple_of(first_ref[0], count), count)

    def next_gram(before):
        once = product(before.astype(BF16), poly_ref[...])
        twice = product(once.astype(BF16), poly_ref[...])
        return NEWTON_A * NEWTON_A * before + 2.0 * NEWTON_A * once + twice

    own_gram = next_gram(gram_ref[rows, :].astype(F32)).astype(BF16)
    squared = next_gram(product(own_gram, gram_ref[...]))
    own_poly = (NEWTON_B * own_gram.astype(F32) + NEWTON_C * squared).astype(BF16)
    weights = NEWTON_A * (poly_ref[rows, :].astype(F32) + own_poly.astype(F32)) + product(own_poly, poly_ref[...])
    result = NEWTON_A * NEWTON_A * x_ref[rows, :].astype(F32) + product(weights.astype(BF16), x_ref[...])
    out_ref[...] = (factor * scale * result).astype(BF16)


def newton_rows(pieces, count, first_row, factor):
    height, width = pieces[0].shape
    size = height * len(pieces)
    square = pltpu.VMEM((size, size), BF16)
    return pl.pallas_call(
        lambda *refs: newton_kernel(count, factor, *refs),
        out_shape=jax.ShapeDtypeStruct((count, width), BF16),
        in_specs=[SCALARS] + [VECTORS] * len(pieces),
        out_specs=VECTORS,
        scratch_shapes=[pltpu.VMEM((size, width), BF16), pltpu.VMEM((size, size), F32), square, square],
        compiler_params=grant(20),
        name="newton",
    )(first_row.reshape(1), *pieces)


def on_device(grads, momentum, owner):
    slots = lax.axis_size("fsdp")
    replicas = lax.axis_size("rep")
    replica = lax.axis_index("rep")
    width = grads.shape[-1]
    lanes = math.gcd(width, 128)
    tiled = (slots, width // lanes, lanes)

    sums = cluster_sums(grads[0], owner, replica, replicas, lanes)
    members = sums.shape[0]
    groups = [[r * slots + s for r in group for s in range(slots)] for group in classes(replicas)]
    terms = lax.all_to_all(
        sums.reshape(members * slots, *tiled[1:]), ("rep", "fsdp"), 0, 0, axis_index_groups=groups, tiled=True
    )
    moment_new, nesterov = momentum_rows(terms.reshape(members, *tiled), momentum.reshape(tiled))

    pieces = gather_rows(nesterov, replicas)
    update_rows = newton_rows(pieces, slots, (replica // (2 * STRIDE)) * slots, math.sqrt(width))

    returning = lax.all_to_all(update_rows.reshape(tiled), "fsdp", split_axis=0, concat_axis=0, tiled=True)
    onehot = (owner[None, :] == jnp.arange(slots, dtype=jnp.int32)[:, None]).astype(BF16)
    updates = jnp.einsum(
        "se,sd->ed", onehot, returning.reshape(slots, width), preferred_element_type=F32
    ).astype(BF16)
    return (updates[:, None, None], moment_new.reshape(momentum.shape))


def solution(mesh):
    placed = (P("rep", None, "fsdp", None), P("fsdp", None, "rep", None), P())
    return jax.shard_map(
        on_device,
        mesh=mesh,
        in_specs=placed,
        out_specs=(P(None, "fsdp", "rep", None), P("fsdp", None, "rep", None)),
        check_vma=False,
    )
```

```python
import math

import jax
import jax.numpy as jnp
from jax import lax
from jax.experimental import pallas as pl
from jax.experimental.pallas import tpu as pltpu
from jax.sharding import PartitionSpec as P

DECAY_RATE = 0.95
NEWTON_A = 3.4445
NEWTON_B = -4.775
NEWTON_C = 2.0315
EPSILON = 1e-07

STRIDE = 3

F32 = jnp.float32
BF16 = jnp.bfloat16

SCALARS = pl.BlockSpec(memory_space=pltpu.SMEM)
VECTORS = pl.BlockSpec(memory_space=pltpu.VMEM)


def grant(mebibytes):
    return pltpu.CompilerParams(vmem_limit_bytes=mebibytes * 2**20)


def neighbours(turn, replicas):
    return [(r, (r + 2 - 4 * ((r + turn) % 2)) % replicas) for r in range(replicas)]


def other_core(replicas):
    return [(r, r ^ 1) for r in range(replicas)]


def classes(replicas):
    chips = replicas // 2
    return [
        [2 * z + core for z in range(first, chips, STRIDE)]
        for first in range(STRIDE)
        for core in range(2)
    ]


def pick(array, index, axis):
    return lax.dynamic_index_in_dim(array, index, axis, keepdims=False)


def chip_sums_kernel(replica_ref, mine_ref, theirs_ref, *out_refs):
    core = lax.rem(replica_ref[0], 2)
    kind = lax.rem(lax.div(replica_ref[0], 2), STRIDE)
    for step, out_ref in zip((1 + core, 2 - core), out_refs, strict=True):
        there = lax.rem(kind + step, STRIDE)
        for n in range(out_ref.shape[0]):
            out_ref[n] = (mine_ref[n, there, core].astype(F32) + theirs_ref[n, there].astype(F32)).astype(BF16)


def cluster_sums_kernel(replica_ref, owner_ref, mine_ref, theirs_ref, first_ref, second_ref, out_ref, row_ref):
    core = lax.rem(replica_ref[0], 2)
    kind = lax.rem(lax.div(replica_ref[0], 2), STRIDE)
    experts, tiles, lanes = row_ref.shape
    for n in range(out_ref.shape[0]):
        total = mine_ref[n, kind, core].astype(F32) + theirs_ref[n, kind].astype(F32)
        total += first_ref[n].astype(F32) + second_ref[n].astype(F32)
        for tile in range(tiles):
            row_ref[:, tile, :] = total[:, tile * lanes : (tile + 1) * lanes]
        for expert in range(experts):
            out_ref[n, owner_ref[expert]] = row_ref[expert].astype(BF16)


def momentum_kernel(terms_ref, moment_ref, moment_out_ref, rows_ref, row_ref):
    total = terms_ref[0].astype(F32)
    for n in range(1, terms_ref.shape[0]):
        total += terms_ref[n].astype(F32)
    moment = DECAY_RATE * moment_ref[...] + total
    moment_out_ref[...] = moment
    row_ref[...] = total + DECAY_RATE * moment
    _, tiles, lanes = row_ref.shape
    for tile in range(tiles):
        rows_ref[:, tile * lanes : (tile + 1) * lanes] = row_ref[:, tile, :].astype(BF16)


def cluster_sums(grads, owner, replica, replicas, lanes):
    experts, _, width = grads.shape
    members = replicas // (2 * STRIDE)
    here = replica.reshape(1)
    mine = grads.transpose(1, 0, 2).reshape(members, STRIDE, 2, experts, width)
    theirs = lax.ppermute(pick(mine, 1 - replica % 2, 2), "rep", other_core(replicas))
    some = jax.ShapeDtypeStruct((members, experts, width), BF16)
    outward = pl.pallas_call(
        chip_sums_kernel,
        out_shape=(some, some),
        in_specs=[SCALARS, VECTORS, VECTORS],
        out_specs=(VECTORS, VECTORS),
        compiler_params=grant(12),
        name="chip_sums",
    )(here, mine, theirs)
    inward = [lax.ppermute(sums, "rep", neighbours(turn, replicas)) for turn, sums in enumerate(outward)]
    tiles = (experts, width // lanes, lanes)
    return pl.pallas_call(
        cluster_sums_kernel,
        out_shape=jax.ShapeDtypeStruct((members, *tiles), BF16),
        in_specs=[SCALARS] * 2 + [VECTORS] * 4,
        out_specs=VECTORS,
        scratch_shapes=[pltpu.VMEM(tiles, F32)],
        compiler_params=grant(12),
        name="cluster_sums",
    )(here, owner, mine, theirs, *inward)


def momentum_rows(terms, moment):
    slots, tiles, lanes = moment.shape
    return pl.pallas_call(
        momentum_kernel,
        out_shape=(jax.ShapeDtypeStruct(moment.shape, F32), jax.ShapeDtypeStruct((slots, tiles * lanes), BF16)),
        in_specs=[VECTORS, VECTORS],
        out_specs=(VECTORS, VECTORS),
        scratch_shapes=[pltpu.VMEM(moment.shape, F32)],
        compiler_params=grant(4),
        name="momentum",
    )(terms, moment)


def gather_rows(rows, replicas):
    own = lax.all_gather(rows, "rep", axis=0, tiled=True, axis_index_groups=classes(replicas))
    near = [lax.ppermute(own, "rep", neighbours(turn, replicas)) for turn in range(2)]
    pieces = [own, *lax.optimization_barrier(near)]
    return pieces + [lax.ppermute(piece, "rep", other_core(replicas)) for piece in pieces]


def product(a, b):
    return lax.dot_general(a, b, (((1,), (0,)), ((), ())), preferred_element_type=F32)


def newton_kernel(count, factor, first_ref, *refs):
    pieces, (out_ref, x_ref, raw_ref, gram_ref, poly_ref) = refs[:-5], refs[-5:]
    height = pieces[0].shape[0]
    for n, piece in enumerate(pieces):
        x_ref[pl.ds(n * height, height), :] = piece[...]
    size = x_ref.shape[0]
    step = 2 * height
    blocks = [pl.ds(n * step, step) for n in range(size // step)]
    diagonal = lax.broadcasted_iota(jnp.int32, (step, step), 0) == lax.broadcasted_iota(jnp.int32, (step, step), 1)
    trace = jnp.float32(0.0)
    for n, block in enumerate(blocks):
        raw = lax.dot_general(x_ref[block, :], x_ref[...], (((1,), (1,)), ((), ())), preferred_element_type=F32)
        raw_ref[block, :] = raw
        trace += jnp.sum(jnp.where(diagonal, raw[:, n * step : (n + 1) * step], 0.0))
    scale = 1.0 / (jnp.sqrt(trace) + EPSILON)
    for block in blocks:
        gram_ref[block, :] = (raw_ref[block, :] * scale * scale).astype(BF16)
    for block in blocks:
        squared = product(gram_ref[block, :], gram_ref[...])
        poly_ref[block, :] = (NEWTON_B * gram_ref[block, :].astype(F32) + NEWTON_C * squared).astype(BF16)
    rows = pl.ds(pl.multiple_of(first_ref[0], count), count)

    def next_gram(before):
        once = product(before.astype(BF16), poly_ref[...])
        twice = product(once.astype(BF16), poly_ref[...])
        return NEWTON_A * NEWTON_A * before + 2.0 * NEWTON_A * once + twice

    own_gram = next_gram(gram_ref[rows, :].astype(F32)).astype(BF16)
    squared = next_gram(product(own_gram, gram_ref[...]))
    own_poly = (NEWTON_B * own_gram.astype(F32) + NEWTON_C * squared).astype(BF16)
    weights = NEWTON_A * (poly_ref[rows, :].astype(F32) + own_poly.astype(F32)) + product(own_poly, poly_ref[...])
    result = NEWTON_A * NEWTON_A * x_ref[rows, :].astype(F32) + product(weights.astype(BF16), x_ref[...])
    out_ref[...] = (factor * scale * result).astype(BF16)


def newton_rows(pieces, count, first_row, factor):
    height, width = pieces[0].shape
    size = height * len(pieces)
    square = pltpu.VMEM((size, size), BF16)
    return pl.pallas_call(
        lambda *refs: newton_kernel(count, factor, *refs),
        out_shape=jax.ShapeDtypeStruct((count, width), BF16),
        in_specs=[SCALARS] + [VECTORS] * len(pieces),
        out_specs=VECTORS,
        scratch_shapes=[pltpu.VMEM((size, width), BF16), pltpu.VMEM((size, size), F32), square, square],
        compiler_params=grant(20),
        name="newton",
    )(first_row.reshape(1), *pieces)


def on_device(grads, momentum, owner):
    slots = lax.axis_size("fsdp")
    replicas = lax.axis_size("rep")
    replica = lax.axis_index("rep")
    width = grads.shape[-1]
    lanes = math.gcd(width, 128)
    tiled = (slots, width // lanes, lanes)

    sums = cluster_sums(grads[0], owner, replica, replicas, lanes)
    members = sums.shape[0]
    groups = [[r * slots + s for r in group for s in range(slots)] for group in classes(replicas)]
    terms = lax.all_to_all(
        sums.reshape(members * slots, *tiled[1:]), ("rep", "fsdp"), 0, 0, axis_index_groups=groups, tiled=True
    )
    moment_new, nesterov = momentum_rows(terms.reshape(members, *tiled), momentum.reshape(tiled))

    pieces = gather_rows(nesterov, replicas)
    update_rows = newton_rows(pieces, slots, (replica // (2 * STRIDE)) * slots, math.sqrt(width))

    returning = lax.all_to_all(update_rows.reshape(tiled), "fsdp", split_axis=0, concat_axis=0, tiled=True)
    onehot = (owner[None, :] == jnp.arange(slots, dtype=jnp.int32)[:, None]).astype(BF16)
    updates = jnp.einsum(
        "se,sd->ed", onehot, returning.reshape(slots, width), preferred_element_type=F32
    ).astype(BF16)
    return (updates[:, None, None], moment_new.reshape(momentum.shape))


def solution(mesh):
    placed = (P("rep", None, "fsdp", None), P("fsdp", None, "rep", None), P())
    return jax.shard_map(
        on_device,
        mesh=mesh,
        in_specs=placed,
        out_specs=(P(None, "fsdp", "rep", None), P("fsdp", None, "rep", None)),
        check_vma=False,
    )
```

```python
import math

import jax
import jax.numpy as jnp
from jax import lax
from jax.experimental import pallas as pl
from jax.experimental.pallas import tpu as pltpu
from jax.sharding import PartitionSpec as P

DECAY_RATE = 0.95
NEWTON_A = 3.4445
NEWTON_B = -4.775
NEWTON_C = 2.0315
EPSILON = 1e-07

STRIDE = 3

F32 = jnp.float32
BF16 = jnp.bfloat16

SCALARS = pl.BlockSpec(memory_space=pltpu.SMEM)
VECTORS = pl.BlockSpec(memory_space=pltpu.VMEM)


def grant(mebibytes):
    return pltpu.CompilerParams(vmem_limit_bytes=mebibytes * 2**20)


def neighbours(turn, replicas):
    return [(r, (r + 2 - 4 * ((r + turn) % 2)) % replicas) for r in range(replicas)]


def other_core(replicas):
    return [(r, r ^ 1) for r in range(replicas)]


def classes(replicas):
    chips = replicas // 2
    return [
        [2 * z + core for z in range(first, chips, STRIDE)]
        for first in range(STRIDE)
        for core in range(2)
    ]


def pick(array, index, axis):
    return lax.dynamic_index_in_dim(array, index, axis, keepdims=False)


def chip_sums_kernel(replica_ref, mine_ref, theirs_ref, *out_refs):
    core = lax.rem(replica_ref[0], 2)
    kind = lax.rem(lax.div(replica_ref[0], 2), STRIDE)
    for step, out_ref in zip((1 + core, 2 - core), out_refs, strict=True):
        there = lax.rem(kind + step, STRIDE)
        for n in range(out_ref.shape[0]):
            out_ref[n] = (mine_ref[n, there, core].astype(F32) + theirs_ref[n, there].astype(F32)).astype(BF16)


def cluster_sums_kernel(replica_ref, owner_ref, mine_ref, theirs_ref, first_ref, second_ref, out_ref, row_ref):
    core = lax.rem(replica_ref[0], 2)
    kind = lax.rem(lax.div(replica_ref[0], 2), STRIDE)
    experts, tiles, lanes = row_ref.shape
    for n in range(out_ref.shape[0]):
        total = mine_ref[n, kind, core].astype(F32) + theirs_ref[n, kind].astype(F32)
        total += first_ref[n].astype(F32) + second_ref[n].astype(F32)
        for tile in range(tiles):
            row_ref[:, tile, :] = total[:, tile * lanes : (tile + 1) * lanes]
        for expert in range(experts):
            out_ref[n, owner_ref[expert]] = row_ref[expert].astype(BF16)


def momentum_kernel(terms_ref, moment_ref, moment_out_ref, rows_ref, row_ref):
    total = terms_ref[0].astype(F32)
    for n in range(1, terms_ref.shape[0]):
        total += terms_ref[n].astype(F32)
    moment = DECAY_RATE * moment_ref[...] + total
    moment_out_ref[...] = moment
    row_ref[...] = total + DECAY_RATE * moment
    _, tiles, lanes = row_ref.shape
    for tile in range(tiles):
        rows_ref[:, tile * lanes : (tile + 1) * lanes] = row_ref[:, tile, :].astype(BF16)


def cluster_sums(grads, owner, replica, replicas, lanes):
    experts, _, width = grads.shape
    members = replicas // (2 * STRIDE)
    here = replica.reshape(1)
    mine = grads.transpose(1, 0, 2).reshape(members, STRIDE, 2, experts, width)
    theirs = lax.ppermute(pick(mine, 1 - replica % 2, 2), "rep", other_core(replicas))
    some = jax.ShapeDtypeStruct((members, experts, width), BF16)
    outward = pl.pallas_call(
        chip_sums_kernel,
        out_shape=(some, some),
        in_specs=[SCALARS, VECTORS, VECTORS],
        out_specs=(VECTORS, VECTORS),
        compiler_params=grant(12),
        name="chip_sums",
    )(here, mine, theirs)
    inward = [lax.ppermute(sums, "rep", neighbours(turn, replicas)) for turn, sums in enumerate(outward)]
    tiles = (experts, width // lanes, lanes)
    return pl.pallas_call(
        cluster_sums_kernel,
        out_shape=jax.ShapeDtypeStruct((members, *tiles), BF16),
        in_specs=[SCALARS] * 2 + [VECTORS] * 4,
        out_specs=VECTORS,
        scratch_shapes=[pltpu.VMEM(tiles, F32)],
        compiler_params=grant(12),
        name="cluster_sums",
    )(here, owner, mine, theirs, *inward)


def momentum_rows(terms, moment):
    slots, tiles, lanes = moment.shape
    return pl.pallas_call(
        momentum_kernel,
        out_shape=(jax.ShapeDtypeStruct(moment.shape, F32), jax.ShapeDtypeStruct((slots, tiles * lanes), BF16)),
        in_specs=[VECTORS, VECTORS],
        out_specs=(VECTORS, VECTORS),
        scratch_shapes=[pltpu.VMEM(moment.shape, F32)],
        compiler_params=grant(4),
        name="momentum",
    )(terms, moment)


def gather_rows(rows, replicas):
    own = lax.all_gather(rows, "rep", axis=0, tiled=True, axis_index_groups=classes(replicas))
    ways = [[(r, (r + way) % replicas) for r in range(replicas)] for way in (2, -2)]
    pieces = [own] + [lax.ppermute(own, "rep", way) for way in ways]
    return pieces + [lax.ppermute(piece, "rep", other_core(replicas)) for piece in pieces]


def product(a, b):
    return lax.dot_general(a, b, (((1,), (0,)), ((), ())), preferred_element_type=F32)


def newton_kernel(count, factor, first_ref, *refs):
    pieces, (out_ref, x_ref, raw_ref, gram_ref, poly_ref) = refs[:-5], refs[-5:]
    height = pieces[0].shape[0]
    for n, piece in enumerate(pieces):
        x_ref[pl.ds(n * height, height), :] = piece[...]
    size = x_ref.shape[0]
    step = 2 * height
    blocks = [pl.ds(n * step, step) for n in range(size // step)]
    diagonal = lax.broadcasted_iota(jnp.int32, (step, step), 0) == lax.broadcasted_iota(jnp.int32, (step, step), 1)
    trace = jnp.float32(0.0)
    for n, block in enumerate(blocks):
        raw = lax.dot_general(x_ref[block, :], x_ref[...], (((1,), (1,)), ((), ())), preferred_element_type=F32)
        raw_ref[block, :] = raw
        trace += jnp.sum(jnp.where(diagonal, raw[:, n * step : (n + 1) * step], 0.0))
    scale = 1.0 / (jnp.sqrt(trace) + EPSILON)
    for block in blocks:
        gram_ref[block, :] = (raw_ref[block, :] * scale * scale).astype(BF16)
    for block in blocks:
        squared = product(gram_ref[block, :], gram_ref[...])
        poly_ref[block, :] = (NEWTON_B * gram_ref[block, :].astype(F32) + NEWTON_C * squared).astype(BF16)
    rows = pl.ds(pl.multiple_of(first_ref[0], count), count)

    def next_gram(before):
        once = product(before.astype(BF16), poly_ref[...])
        twice = product(once.astype(BF16), poly_ref[...])
        return NEWTON_A * NEWTON_A * before + 2.0 * NEWTON_A * once + twice

    own_gram = next_gram(gram_ref[rows, :].astype(F32)).astype(BF16)
    squared = next_gram(product(own_gram, gram_ref[...]))
    own_poly = (NEWTON_B * own_gram.astype(F32) + NEWTON_C * squared).astype(BF16)
    weights = NEWTON_A * (poly_ref[rows, :].astype(F32) + own_poly.astype(F32)) + product(own_poly, poly_ref[...])
    result = NEWTON_A * NEWTON_A * x_ref[rows, :].astype(F32) + product(weights.astype(BF16), x_ref[...])
    out_ref[...] = (factor * scale * result).astype(BF16)


def newton_rows(pieces, count, first_row, factor):
    height, width = pieces[0].shape
    size = height * len(pieces)
    square = pltpu.VMEM((size, size), BF16)
    return pl.pallas_call(
        lambda *refs: newton_kernel(count, factor, *refs),
        out_shape=jax.ShapeDtypeStruct((count, width), BF16),
        in_specs=[SCALARS] + [VECTORS] * len(pieces),
        out_specs=VECTORS,
        scratch_shapes=[pltpu.VMEM((size, width), BF16), pltpu.VMEM((size, size), F32), square, square],
        compiler_params=grant(20),
        name="newton",
    )(first_row.reshape(1), *pieces)


def on_device(grads, momentum, owner):
    slots = lax.axis_size("fsdp")
    replicas = lax.axis_size("rep")
    replica = lax.axis_index("rep")
    width = grads.shape[-1]
    lanes = math.gcd(width, 128)
    tiled = (slots, width // lanes, lanes)

    sums = cluster_sums(grads[0], owner, replica, replicas, lanes)
    members = sums.shape[0]
    groups = [[r * slots + s for r in group for s in range(slots)] for group in classes(replicas)]
    terms = lax.all_to_all(
        sums.reshape(members * slots, *tiled[1:]), ("rep", "fsdp"), 0, 0, axis_index_groups=groups, tiled=True
    )
    moment_new, nesterov = momentum_rows(terms.reshape(members, *tiled), momentum.reshape(tiled))

    pieces = gather_rows(nesterov, replicas)
    update_rows = newton_rows(pieces, slots, (replica // (2 * STRIDE)) * slots, math.sqrt(width))

    returning = lax.all_to_all(update_rows.reshape(tiled), "fsdp", split_axis=0, concat_axis=0, tiled=True)
    onehot = (owner[None, :] == jnp.arange(slots, dtype=jnp.int32)[:, None]).astype(BF16)
    updates = jnp.einsum(
        "se,sd->ed", onehot, returning.reshape(slots, width), preferred_element_type=F32
    ).astype(BF16)
    return (updates[:, None, None], moment_new.reshape(momentum.shape))


def solution(mesh):
    placed = (P("rep", None, "fsdp", None), P("fsdp", None, "rep", None), P())
    return jax.shard_map(
        on_device,
        mesh=mesh,
        in_specs=placed,
        out_specs=(P(None, "fsdp", "rep", None), P("fsdp", None, "rep", None)),
        check_vma=False,
    )
```
